256 devices in a mesh: expert: 32 (over z, y), dp: 8 (over x, core).
Axes of the slice: x: 4, y: 4, z: 8, core: 2. Of those that a mesh axis runs over, the one named last changes fastest.
Arguments:
- tokens: bfloat16 [8192, 4096], P(('expert', 'dp')), may hold values from -6 to 6
- out_grad: bfloat16 [8192, 4096], P(('expert', 'dp')), may hold values from -6 to 6
- gate_probs: bfloat16 [8192, 8], P(('expert', 'dp')), may hold values from 0.049804688 to 0.5
- route_ids: int32 [8192, 8], P(('expert', 'dp')), may hold values from 0 to 127, all different within a row; in each aligned block of 32 rows (0 to 31, 32 to 63, ...) at most 4 rows name the same one
- w_gate: bfloat16 [32, 1536, 4096], P('expert', 'dp'), may hold values from -0.09375 to 0.09375
- w_up: bfloat16 [32, 1536, 4096], P('expert', 'dp'), may hold values from -0.09375 to 0.09375
- w_down: bfloat16 [32, 1536, 4096], P('expert', 'dp'), may hold values from -0.15625 to 0.15625
Outputs:
- token_grad: bfloat16 [8192, 4096], P(('expert', 'dp'))
- gate_grad: float32 [8192, 8], P(('expert', 'dp'))
- grad_gate: bfloat16 [32, 1536, 4096], P('expert', 'dp')
- grad_up: bfloat16 [32, 1536, 4096], P('expert', 'dp')
- grad_down: bfloat16 [32, 1536, 4096], P('expert', 'dp')
The draws below stay inside these ranges and needn't reach their ends.
Inputs may be any that keep to these rules, and one draw needn't show every extreme that they name: `route_ids`: the 8 ids of a token differ. In each aligned block of 32 rows (the tokens of one device) no id is named by more than 4 rows, a bound that some block reaches.
All inputs are finite; a program needn't handle non-finite values.
Results may differ from the reference program's by a relative error of at most 0.014.
Values may be sent and summed in bfloat16 or wider, within the bound.
A program may use at most 128 MiB of HBM per device.

```python
import math
import jax
import jax.numpy as jnp
import numpy as np
from jax import lax

D = 4096
FF = 1536
EXPERTS = 128
TOPK = 8
TOK_DEV = 32
CAP = 4
WINDOW = 32
TOKENS = 8192
N_EXPERT = 32
N_DP = 8


def block_scale(key, extent, cuts, low, top_value):
    loudness = 1.0
    for dim, parts in cuts:
        heights = jax.random.uniform(jax.random.fold_in(jax.random.fold_in(key, 6), dim), (parts,), jnp.float32, low / len(cuts), top_value / len(cuts))
        loudness = loudness * jnp.repeat(jnp.exp(heights), extent[dim] // parts).reshape((-1,) + (1,) * (len(extent) - 1 - dim))
    return loudness


def assign_block(key, own, number, rows, number_of, top, bound, skew):
    ranking = jax.random.permutation(key, number_of)
    crowded, usual = portions_of(number_of, rows * top, bound, skew, True), portions_of(number_of, rows * top, bound, skew, False)
    places = jnp.arange(number_of)

    def named(tallies, turn):
        used = int((tallies > 0).sum())
        fixed = max(1, used // 4)
        shifted = fixed + (places - fixed + turn * (used - fixed)) % max(1, number_of - fixed)
        return jnp.zeros((number_of,), jnp.int32).at[ranking[jnp.where(places < fixed, places, shifted)]].set(jnp.asarray(tallies, jnp.int32))

    tallies = jnp.where(number % 4 == 0, named(crowded, number // 4), named(usual, number - number // 4 - 1))
    mixed = jax.random.permutation(jax.random.fold_in(own, 3), number_of)
    donor, sink = mixed[0:number_of // 2 * 2:2], mixed[1:number_of // 2 * 2:2]
    slack = jnp.minimum(tallies[donor] - 1, bound - tallies[sink]) // 2
    slack = jnp.where((donor == ranking[0]) | (sink == ranking[0]) | (tallies[sink] == 0), 0, jnp.maximum(slack, 0))
    shifted = jax.random.randint(jax.random.fold_in(own, 4), (number_of // 2,), 0, 1 << 20) % (slack + 1)
    tallies = tallies.at[donor].add(-shifted).at[sink].add(shifted)
    labels = jnp.searchsorted(jnp.cumsum(tallies), jnp.arange(rows * top), side="right").astype(jnp.int32)
    grid = labels.reshape(top, rows).T
    grid = grid[jax.random.permutation(jax.random.fold_in(own, 1), rows)]
    turn = jax.random.randint(jax.random.fold_in(own, 2), (rows, 1), 0, top)
    return jnp.take_along_axis(grid, (jnp.arange(top)[None, :] + turn) % top, axis=1)


def portions_of(amount, total, bound, lean, full):
    weights = [(1 << 20) // math.isqrt(grade ** lean) + 1 for grade in range(1, amount + 1)]
    largest = bound if full else min(bound, max(-(-total // amount), total * weights[0] // sum(weights)))
    least = 1 if total - largest >= amount - 1 else 0
    given, surplus = [largest] + [least] * (amount - 1), total - largest - least * (amount - 1)
    while surplus > 0:
        candidates = [i for i in range(1, amount) if given[i] < largest] or [i for i in range(1, amount) if given[i] < bound]
        pool, left = sum([weights[i] for i in candidates]), surplus
        for i in candidates:
            more = min(bound - given[i], max(1, left * weights[i] // pool), surplus)
            given[i] = given[i] + more
            surplus = surplus - more
    return np.array(given)


def bell_draw(key, shape, deviation, most, split=(), kind=jnp.bfloat16):
    entries = jax.random.normal(key, shape, jnp.float32) * deviation
    if len(split) > 0:
        entries = block_scale(key, shape, split, -0.22, 0.18) * entries
    return jnp.clip(entries, min=-most, max=most).astype(kind)


def setup_inputs(seed: int = 0) -> dict:
    streams_of = jax.random.split(jax.random.key(seed), 8)
    tokens = bell_draw(streams_of[0], (TOKENS, D), 1.0, 6.0, ((0, 256),))
    out_grad = bell_draw(streams_of[1], (TOKENS, D), 1.0, 6.0, ((0, 256),))
    gate_probs = jnp.clip(jnp.exp(math.log(0.5) - 2.306499 * jax.random.uniform(streams_of[2], (TOKENS, TOPK), jnp.float32) ** block_scale(streams_of[2], (TOKENS, TOPK), ((0, 256),), -0.2, 0.2)), 0.049804688, 0.5).astype(jnp.bfloat16)
    route_ids_keys = jax.random.split(jax.random.fold_in(streams_of[3], 1), TOKENS // TOK_DEV)
    route_ids_turns = jax.random.permutation(jax.random.fold_in(streams_of[3], 3), TOKENS // TOK_DEV)
    route_ids = jax.vmap(lambda own, number: assign_block(jax.random.fold_in(streams_of[3], 2), own, number, TOK_DEV, EXPERTS, TOPK, CAP, 2))(route_ids_keys, route_ids_turns).reshape((TOKENS, TOPK))
    w_gate = bell_draw(streams_of[4], (WINDOW, FF, D), D ** -0.5, 0.09375, ((0, 32), (1, 8)))
    w_up = bell_draw(streams_of[5], (WINDOW, FF, D), D ** -0.5, 0.09375, ((0, 32), (1, 8)))
    w_down = bell_draw(streams_of[6], (WINDOW, FF, D), FF ** -0.5, 0.15625, ((0, 32), (1, 8)))
    return {"tokens": tokens, "out_grad": out_grad, "gate_probs": gate_probs, "route_ids": route_ids, "w_gate": w_gate, "w_up": w_up, "w_down": w_down}


def reference(tokens, out_grad, gate_probs, route_ids, w_gate, w_up, w_down):
    token_total, model_width = tokens.shape
    top_count = route_ids.shape[1]
    pair_total = token_total * top_count
    hidden_units = w_gate.shape[1]
    group_units = hidden_units // N_DP
    per_device = EXPERTS // N_EXPERT
    room = N_EXPERT * N_DP * CAP
    flat_ids = route_ids.reshape(-1)
    active = (flat_ids % per_device) == 0
    target = jnp.where(active, flat_ids // per_device, N_EXPERT).astype(jnp.int32)
    onehot = (target[:, None] == jnp.arange(N_EXPERT, dtype=jnp.int32)[None, :]).astype(jnp.int32)
    slot_rank = jnp.sum((jnp.cumsum(onehot, axis=0) - onehot) * onehot, axis=1).astype(jnp.int32)
    place = jnp.where(active, target * room + slot_rank, N_EXPERT * room).astype(jnp.int32)
    pair_owner = jnp.full((N_EXPERT * room + 1,), pair_total, jnp.int32)
    pair_owner = pair_owner.at[place].set(jnp.arange(pair_total, dtype=jnp.int32))
    pair_owner = pair_owner[: N_EXPERT * room].reshape(N_EXPERT, room)
    gates_flat = gate_probs.reshape(-1).astype(jnp.float32)

    def one_expert(totals, inputs):
        token_acc, gate_acc = totals
        pair_index, gate_weight, up_weight, down_weight = inputs
        occupied = pair_index < pair_total
        safe_index = jnp.where(occupied, pair_index, 0).astype(jnp.int32)
        token_index = (safe_index // top_count).astype(jnp.int32)
        row_tokens = jnp.where(occupied[:, None], tokens[token_index], jnp.zeros_like(tokens[token_index]))
        row_grads = jnp.where(occupied[:, None], out_grad[token_index], jnp.zeros_like(out_grad[token_index]))
        row_gates = jnp.where(occupied, gates_flat[safe_index], jnp.float32(0.0))
        pre_gate = jnp.dot(row_tokens, gate_weight.T, preferred_element_type=jnp.float32)
        pre_up = jnp.dot(row_tokens, up_weight.T, preferred_element_type=jnp.float32)
        back_proj = jnp.dot(row_grads, down_weight.T, preferred_element_type=jnp.float32)
        squash = jax.nn.sigmoid(pre_gate)
        activated = pre_gate * squash
        hidden = (activated * pre_up).astype(jnp.bfloat16)
        gate_terms = jnp.sum(hidden.astype(jnp.float32) * back_proj, axis=1)
        out_scaled = (row_gates[:, None] * row_grads.astype(jnp.float32)).astype(jnp.bfloat16)
        hidden_grad = row_gates[:, None] * back_proj
        up_pre_grad = (hidden_grad * activated).astype(jnp.bfloat16)
        gate_pre_grad = (hidden_grad * pre_up * squash * (1.0 + pre_gate * (1.0 - squash))).astype(jnp.bfloat16)
        grad_down = jnp.dot(hidden.T, out_scaled, preferred_element_type=jnp.float32).astype(jnp.bfloat16)
        grad_gate = jnp.dot(gate_pre_grad.T, row_tokens, preferred_element_type=jnp.float32).astype(jnp.bfloat16)
        grad_up = jnp.dot(up_pre_grad.T, row_tokens, preferred_element_type=jnp.float32).astype(jnp.bfloat16)
        pair_grad = jnp.zeros((room, model_width), jnp.float32)
        for member in range(N_DP):
            low_unit = member * group_units
            high_unit = low_unit + group_units
            partial_value = jnp.dot(gate_pre_grad[:, low_unit:high_unit], gate_weight[low_unit:high_unit], preferred_element_type=jnp.float32)
            partial_value = partial_value + jnp.dot(up_pre_grad[:, low_unit:high_unit], up_weight[low_unit:high_unit], preferred_element_type=jnp.float32)
            rounded = lax.optimization_barrier(partial_value.astype(jnp.bfloat16))
            pair_grad = pair_grad + rounded.astype(jnp.float32)
        pair_grad = jnp.where(occupied[:, None], pair_grad, jnp.float32(0.0))
        token_acc = token_acc.at[token_index].add(pair_grad)
        drop_index = jnp.where(occupied, pair_index, pair_total).astype(jnp.int32)
        gate_acc = gate_acc.at[drop_index].add(gate_terms, mode="drop")
        return (token_acc, gate_acc), (grad_gate, grad_up, grad_down)

    initial = (jnp.zeros((token_total, model_width), jnp.float32), jnp.zeros((pair_total,), jnp.float32))
    finals, weight_grads = lax.scan(one_expert, initial, (pair_owner, w_gate, w_up, w_down))
    token_acc, gate_acc = finals
    return (token_acc.astype(jnp.bfloat16), gate_acc.reshape(token_total, top_count), weight_grads[0], weight_grads[1], weight_grads[2])
```

```python
import jax
import jax.numpy as jnp
from jax import lax
from jax.experimental import pallas as pl
from jax.experimental.pallas import tpu as pltpu
from jax.sharding import PartitionSpec as P

EXPERTS = 128
CAP = 4
NX = 4
NC = 2
NY = 4
CHUNKS = 8
LANES = 128
MESH = pl.DeviceIdType.MESH
LAST = (((1,), (1,)), ((), ()))
F32 = jnp.float32
BF16 = jnp.bfloat16


def mm(a, b):
    return jnp.dot(a, b, preferred_element_type=F32)


def mm_t(a, b):
    return lax.dot_general(a, b, LAST, preferred_element_type=F32)


def rows_of(index, size):
    return pl.ds(pl.multiple_of(index * size, size), size)


def kernel(
    nz, tok, og, pp, wg, wu, wd,
    tg_out, ext_out, gg_out, gu_out, gd_out,
    pb, pm, pgm, ptm, ty, zs, xg, ww, acc, gp, up, hd, gpt, upt, hdt,
    ps, pk, pr, hl, hr, fl, fr, rs, rz, ts, tr, go,
    pse, pke, pre, hle, hre, fle, fre, rse, rze, tse, tre,
    s_p, s_y, s_z, s_xl, s_xr, s_fl, s_fr, s_c, s_w,
    t_p, t_y, t_z, t_x,
    r_c, r_hl, r_hr, r_fl, r_fr, r_z, r_y,
    u_c, u_h, u_f, u_z, u_y, u_o,
):
    chunks, _, block_tokens, width = ty.shape
    toks = block_tokens // NY
    unit = NY * CAP
    block = nz * unit
    half = block // 2
    column = NX * block
    e = lax.axis_index("expert")
    m = lax.axis_index("dp")
    z, y = e // NY, lax.rem(e, NY)
    x, core = m // NC, lax.rem(m, NC)
    other = 1 - core
    xr, xl, xo = lax.rem(x + 1, NX), lax.rem(x + NX - 1, NX), lax.rem(x + 2, NX)
    right, left, partner = (e, xr * NC + core), (e, xl * NC + core), (e, x * NC + other)
    y_peers = [lax.rem(y + d, NY) for d in range(1, NY)]
    z_peers = [lax.rem(z + d, nz) for d in range(1, nz)]

    def at_y(v):
        return (z * NY + v, m)

    def at_z(v):
        return (v * NY + y, m)

    def send(src, dst, ssem, rsem, dev):
        pltpu.make_async_remote_copy(
            src_ref=src, dst_ref=dst, send_sem=ssem, recv_sem=rsem,
            device_id=dev, device_id_type=MESH,
        ).start()

    def local(src, dst, sem):
        pltpu.make_async_copy(src, dst, sem).start()

    def take(ref, sem):
        pltpu.make_async_copy(ref, ref, sem).wait()

    barrier = pltpu.get_barrier_semaphore()
    peers = [at_y(v) for v in y_peers] + [at_z(v) for v in z_peers] + [right, left, partner]
    for dev in peers:
        pl.semaphore_signal(barrier, inc=1, device_id=dev, device_id_type=MESH)
    pl.semaphore_wait(barrier, len(peers))

    for v in y_peers:
        send(pp.at[v], pb.at[y], t_p, s_p, at_y(v))
    local(pp.at[y], pb.at[y], s_p)

    @pl.loop(0, chunks)
    def _(c):
        cols = rows_of(c, width)
        mine = rows_of(y, toks)
        for a, src in enumerate((tok, og)):
            for v in y_peers:
                send(src.at[:, cols], ty.at[c, a, mine], t_y.at[c], s_y.at[c], at_y(v))
            local(src.at[:, cols], ty.at[c, a, mine], s_y.at[c])

    @pl.loop(0, chunks)
    def _(c):
        cols = rows_of(c, width)
        for i, src in enumerate((wg, wu, wd)):
            local(src.at[:, cols], ww.at[c, i], s_w)

    take(pb, s_p)
    total = pb[0].astype(F32)
    for v in range(1, NY):
        total = total + pb[v].astype(F32)
    pm[...] = total[0].astype(BF16)
    pgm[...] = total[1].astype(BF16)
    ptm[...] = total[0].T.astype(BF16)
    acc[...] = jnp.zeros_like(acc)

    mine_rows = rows_of(core * NX + x, block)
    left_rows = rows_of(core * NX + xl, block)
    right_rows = rows_of(core * NX + xr, block)
    opp_rows = rows_of(core * NX + xo, block)
    opp_0 = rows_of((core * NX + xo) * 2, half)
    opp_1 = rows_of((core * NX + xo) * 2 + 1, half)
    left_0 = rows_of((core * NX + xl) * 2, half)
    right_1 = rows_of((core * NX + xr) * 2 + 1, half)
    my_unit = rows_of(z, unit)

    def stage_z(c):
        take(ty.at[c], s_y.at[c])
        zs[c, 0] = mm(pm[...], ty[c, 0]).astype(BF16)
        zs[c, 1] = mm(pgm[...], ty[c, 1]).astype(BF16)
        dst = xg.at[c, :, rows_of((core * NX + x) * nz + z, unit)]
        for v in z_peers:
            send(zs.at[c, :, rows_of(v, unit)], dst, t_z.at[c], s_z.at[c], at_z(v))
        local(zs.at[c, :, my_unit], dst, s_z.at[c])

    def stage_x(c):
        own = xg.at[c, :, mine_rows]
        take(own, s_z.at[c])
        send(own, own, t_x.at[c], s_xl.at[c], right)
        send(own, own, t_x.at[c], s_xr.at[c], left)
        send(own, own, t_x.at[c], s_c.at[c], partner)

    def stage_x2(c):
        from_left = xg.at[c, :, left_rows]
        take(from_left, s_xl.at[c])
        part = xg.at[c, :, left_0]
        send(part, part, t_x.at[c], s_fl.at[c], right)
        send(from_left, from_left, t_x.at[c], s_c.at[c], partner)
        from_right = xg.at[c, :, right_rows]
        take(from_right, s_xr.at[c])
        part = xg.at[c, :, right_1]
        send(part, part, t_x.at[c], s_fr.at[c], left)
        send(from_right, from_right, t_x.at[c], s_c.at[c], partner)

    def stage_x3(c):
        take(xg.at[c, :, opp_0], s_fl.at[c])
        take(xg.at[c, :, opp_1], s_fr.at[c])
        opp = xg.at[c, :, opp_rows]
        send(opp, opp, t_x.at[c], s_c.at[c], partner)

    def stage_f(c):
        @pl.when(c == 0)
        def _():
            take(ww, s_w)

        take(xg.at[c, :, rows_of(other, column)], s_c.at[c])

        @pl.loop(0, NC * NX // 2)
        def _(b):
            rows = rows_of(b, 2 * block)
            xs = xg[c, 0, rows]
            acc[0, rows] += mm_t(xs, ww[c, 0])
            acc[1, rows] += mm_t(xs, ww[c, 1])
            acc[2, rows] += mm_t(xg[c, 1, rows], ww[c, 2])

    stages = (stage_z, stage_x, stage_x2, stage_x3, stage_f)

    @pl.loop(0, chunks + len(stages) - 1)
    def _(t):
        for lag, stage in enumerate(stages):
            c = t - lag

            @pl.when(jnp.logical_and(c >= 0, c < chunks))
            def _(stage=stage, c=c):
                stage(c)

    def activate(rows):
        pre_gate, pre_up, hidden_grad = acc[0, rows], acc[1, rows], acc[2, rows]
        squash = jax.nn.sigmoid(pre_gate)
        activated = pre_gate * squash
        hidden = (activated * pre_up).astype(BF16)
        terms = jnp.sum(hidden.astype(F32) * hidden_grad, axis=1, keepdims=True)
        up_grad = hidden_grad * activated
        gate_grad = hidden_grad * pre_up * squash * (1.0 + pre_gate * (1.0 - squash))
        gp[rows] = gate_grad.astype(BF16)
        up[rows] = up_grad.astype(BF16)
        hd[rows] = hidden
        lane = lax.broadcasted_iota(jnp.int32, (block, LANES), 1)
        return jnp.where(lane == e, terms, 0.0).astype(BF16)

    @pl.loop(0, NX)
    def _(b):
        pse[rows_of(b, block)] = activate(rows_of(other * NX + b, block))
        pke[rows_of(b, block)] = activate(rows_of(core * NX + b, block))

    main = (ps, pk, pr, hl, hr, fl, fr, rs, rz, ts, tr)
    extra = (pse, pke, pre, hle, hre, fle, fre, rse, rze, tse, tre)

    def pick(refs, c):
        return [r.at[c] for r in refs] if refs is main else list(refs)

    def to_partner(refs, c):
        b = pick(refs, c)
        send(b[0], b[2], u_c.at[c], r_c.at[c], partner)

    def stage_pair(c):
        rows = rows_of(other, column)
        ps[c] = (mm(gp[rows], ww[c, 0]) + mm(up[rows], ww[c, 1])).astype(BF16)
        to_partner(main, c)
        rows = rows_of(core, column)
        pk[c] = (mm(gp[rows], ww[c, 0]) + mm(up[rows], ww[c, 1])).astype(BF16)

    def stage_r1(refs, c):
        _, keep, came, to_l, to_r, *_ = pick(refs, c)
        take(came, r_c.at[c])

        @pl.loop(0, NX)
        def _(b):
            rows = rows_of(b, block)
            keep[rows] = (keep[rows].astype(F32) + came[rows].astype(F32)).astype(BF16)

        send(keep.at[rows_of(xo * 2, half)], to_l, u_h.at[c], r_hl.at[c], right)
        send(keep.at[rows_of(xo * 2 + 1, half)], to_r, u_h.at[c], r_hr.at[c], left)

    def stage_r2(refs, c):
        _, keep, _, half_l, half_r, full_l, full_r, *_ = pick(refs, c)
        take(half_l, r_hl.at[c])
        rows = rows_of(xr * 2, half)
        keep[rows] = (keep[rows].astype(F32) + half_l[...].astype(F32)).astype(BF16)
        send(keep.at[rows_of(xr, block)], full_l, u_f.at[c], r_fl.at[c], right)
        take(half_r, r_hr.at[c])
        rows = rows_of(xl * 2 + 1, half)
        keep[rows] = (keep[rows].astype(F32) + half_r[...].astype(F32)).astype(BF16)
        send(keep.at[rows_of(xl, block)], full_r, u_f.at[c], r_fr.at[c], left)

    def stage_r3(refs, c):
        _, keep, _, _, _, full_l, full_r, done, back, *_ = pick(refs, c)
        take(full_l, r_fl.at[c])
        take(full_r, r_fr.at[c])
        done[...] = (
            keep[rows_of(x, block)].astype(F32)
            + full_l[...].astype(F32)
            + full_r[...].astype(F32)
        ).astype(BF16)
        for v in z_peers:
            send(done.at[rows_of(v, unit)], back.at[my_unit], u_z.at[c], r_z.at[c], at_z(v))
        local(done.at[my_unit], back.at[my_unit], r_z.at[c])

    def stage_r4(refs, c):
        *_, back, parts, summed = pick(refs, c)
        take(back, r_z.at[c])
        parts[...] = mm(ptm[...], back[...]).astype(BF16)
        mine = rows_of(y, toks)
        for v in y_peers:
            send(parts.at[rows_of(v, toks)], summed.at[mine], u_y.at[c], r_y.at[c], at_y(v))
        local(parts.at[mine], summed.at[mine], r_y.at[c])

    def stage_r5(refs, c):
        summed = pick(refs, c)[-1]
        take(summed, r_y.at[c])
        out = summed[pl.ds(0, toks)].astype(F32)
        for v in range(1, NY):
            out = out + summed[pl.ds(v * toks, toks)].astype(F32)
        if refs is main:
            tg_out[:, rows_of(c, width)] = out.astype(BF16)
        else:
            ext_out[...] = out

    def transposes():
        for src, dst in ((gp, gpt), (up, upt), (hd, hdt)):
            @pl.loop(0, NC * NX)
            def _(b, src=src, dst=dst):
                rows = rows_of(b, block)
                dst[:, rows] = src[rows].astype(F32).T.astype(BF16)

    def weight_grads(c):
        cols = rows_of(c, width)
        tokens_c = xg[c, 0]
        go[c, 0] = mm(gpt[...], tokens_c).astype(BF16)
        go[c, 1] = mm(upt[...], tokens_c).astype(BF16)
        go[c, 2] = mm(hdt[...], xg[c, 1]).astype(BF16)
        for i, dst in enumerate((gg_out, gu_out, gd_out)):
            local(go.at[c, i], dst.at[0, :, cols], u_o.at[c, i])

    to_partner(extra, chunks)
    returns = (stage_r1, stage_r2, stage_r3, stage_r4, stage_r5)

    @pl.loop(0, chunks + len(returns))
    def _(t):
        @pl.when(t < chunks)
        def _():
            stage_pair(t)

        for lag, stage in enumerate(returns):
            @pl.when(t == lag)
            def _(stage=stage):
                stage(extra, chunks)

            c = t - lag - 1

            @pl.when(jnp.logical_and(c >= 0, c < chunks))
            def _(stage=stage, c=c):
                stage(main, c)

        @pl.when(t == 0)
        def _():
            transposes()

        @pl.when(t < chunks)
        def _():
            weight_grads(t)

    take(pb.at[pl.ds(1, NY - 1)], t_p)

    def drain(refs, c):
        b = pick(refs, c)
        take(b[0], u_c.at[c])
        take(b[5], u_h.at[c])
        take(b[1].at[pl.ds(0, 2 * block)], u_f.at[c])
        take(b[8].at[pl.ds(0, block - unit)], u_z.at[c])
        take(b[10].at[pl.ds(0, block_tokens - toks)], u_y.at[c])

    drain(extra, chunks)

    @pl.loop(0, chunks)
    def _(c):
        take(ty.at[c, :, pl.ds(0, block_tokens - toks)], t_y.at[c])
        take(zs.at[c, :, pl.ds(0, block - unit)], t_z.at[c])
        take(xg.at[c, :, pl.ds(0, 7 * block)], t_x.at[c])
        drain(main, c)
        cols = rows_of(c, width)
        for i, dst in enumerate((gg_out, gu_out, gd_out)):
            pltpu.make_async_copy(go.at[c, i], dst.at[0, :, cols], u_o.at[c, i]).wait()


def run(tokens, out_grad, pp, w_gate, w_up, w_down, nz):
    toks, depth = tokens.shape
    units = w_gate.shape[0]
    chunks = CHUNKS
    width = depth // chunks
    block = nz * NY * CAP
    total = block * NX * NC
    column = block * NX
    any_spec = pl.BlockSpec(memory_space=pl.ANY)
    vmem_spec = pl.BlockSpec(memory_space=pltpu.VMEM)
    dma = pltpu.SemaphoreType.DMA
    v = pltpu.VMEM

    def back(lead, w):
        return [
            v(lead + (column, w), BF16),
            v(lead + (column, w), BF16),
            v(lead + (column, w), BF16),
            v(lead + (block // 2, w), BF16),
            v(lead + (block // 2, w), BF16),
            v(lead + (block, w), BF16),
            v(lead + (block, w), BF16),
            v(lead + (block, w), BF16),
            v(lead + (block, w), BF16),
            v(lead + (NY * toks, w), BF16),
            v(lead + (NY * toks, w), BF16),
        ]

    scratch = [
        v((NY, 2, block, NY * toks), BF16),
        v((block, NY * toks), BF16),
        v((block, NY * toks), BF16),
        v((NY * toks, block), BF16),
        v((chunks, 2, NY * toks, width), BF16),
        v((chunks, 2, block, width), BF16),
        v((chunks, 2, total, width), BF16),
        v((chunks, 3, units, width), BF16),
        v((3, total, units), F32),
        v((total, units), BF16),
        v((total, units), BF16),
        v((total, units), BF16),
        v((units, total), BF16),
        v((units, total), BF16),
        v((units, total), BF16),
        *back((chunks,), width),
        v((chunks, 3, units, width), BF16),
        *back((), LANES),
        dma(()), *[dma((chunks,)) for _ in range(7)], dma(()),
        dma(()), *[dma((chunks,)) for _ in range(3)],
        *[dma((chunks + 1,)) for _ in range(7)],
        *[dma((chunks + 1,)) for _ in range(5)],
        dma((chunks, 3)),
    ]
    grads = jax.ShapeDtypeStruct((1, units, depth), BF16)

    def body(*refs):
        kernel(nz, *refs)

    return pl.pallas_call(
        body,
        out_shape=(
            jax.ShapeDtypeStruct((toks, depth), BF16),
            jax.ShapeDtypeStruct((toks, LANES), F32),
            grads, grads, grads,
        ),
        in_specs=[any_spec] * 6,
        out_specs=(vmem_spec, vmem_spec, any_spec, any_spec, any_spec),
        scratch_shapes=scratch,
        compiler_params=pltpu.CompilerParams(
            collective_id=0, has_side_effects=True, vmem_limit_bytes=67043328
        ),
    )(tokens, out_grad, pp, w_gate, w_up, w_down)


def body(tokens, out_grad, gate_probs, route_ids, w_gate, w_up, w_down):
    n_targets = lax.axis_size("expert")
    nz = n_targets // NY
    toks = tokens.shape[0]
    per_device = EXPERTS // n_targets
    y = lax.rem(lax.axis_index("expert"), NY)
    gates = gate_probs.astype(F32)
    named = route_ids[:, :, None] == per_device * jnp.arange(n_targets, dtype=jnp.int32)
    active = jnp.any(named, axis=1).astype(F32)
    weight = jnp.sum(jnp.where(named, gates[:, :, None], 0.0), axis=1)
    order = jnp.arange(toks)
    before = (order[:, None] > order[None, :]).astype(F32)
    rank = jnp.dot(before, active, preferred_element_type=F32)
    placed = jnp.logical_and(
        active.T[:, None, :] > 0.0,
        rank.T[:, None, :] == jnp.arange(CAP, dtype=F32)[None, :, None],
    )
    one = placed.astype(F32)
    scaled = jnp.where(placed, weight.T[:, None, :], 0.0)
    both = jnp.stack([one, scaled]).reshape(2, nz, NY, CAP, toks)
    mine = (jnp.arange(NY) == y).astype(F32)
    spread = (
        both.transpose(2, 0, 1, 3, 4)[:, :, :, None, :, None, :]
        * mine[None, None, None, :, None, None, None]
        * mine[None, None, None, None, None, :, None]
    )
    pp = spread.reshape(NY, 2, nz * NY * CAP, NY * toks).astype(BF16)
    token_grad, ext, grad_gate, grad_up, grad_down = run(
        tokens, out_grad, pp, w_gate[0], w_up[0], w_down[0], nz
    )
    values = jnp.sum(jnp.where(named, ext[:, None, :n_targets], 0.0), axis=2)
    return token_grad, values / gates, grad_gate, grad_up, grad_down


def solution(mesh):
    in_specs = (
        P(("expert", "dp"), None),
        P(("expert", "dp"), None),
        P(("expert", "dp"), None),
        P(("expert", "dp"), None),
        P("expert", "dp", None),
        P("expert", "dp", None),
        P("expert", "dp", None),
    )
    out_specs = (
        P(("expert", "dp"), None),
        P(("expert", "dp"), None),
        P("expert", "dp", None),
        P("expert", "dp", None),
        P("expert", "dp", None),
    )
    return jax.shard_map(body, mesh=mesh, in_specs=in_specs, out_specs=out_specs, check_vma=False)
```

```python
import jax
import jax.numpy as jnp
from jax import lax
from jax.experimental import pallas as pl
from jax.experimental.pallas import tpu as pltpu
from jax.sharding import PartitionSpec as P

EXPERTS = 128
CAP = 4
NX = 4
NC = 2
NY = 4
CHUNKS = 8
LANES = 128
MESH = pl.DeviceIdType.MESH
LAST = (((1,), (1,)), ((), ()))
F32 = jnp.float32
BF16 = jnp.bfloat16


def mm(a, b):
    return jnp.dot(a, b, preferred_element_type=F32)


def mm_t(a, b):
    return lax.dot_general(a, b, LAST, preferred_element_type=F32)


def rows_of(index, size):
    return pl.ds(pl.multiple_of(index * size, size), size)


def kernel(
    nz, tok, og, idt, gpr, wg, wu, wd,
    tg_out, gate_out, gg_out, gu_out, gd_out,
    pp, pb, pm, pgm, ptm, ty, zs, xg, ww, acc, gp, up, hd, gpt, upt, hdt,
    ps, pk, pr, hl, hr, fl, fr, rs, rz, ts, tr, go,
    pse, pke, pre, hle, hre, fle, fre, rse, rze, tse, tre,
    s_p, s_y, s_z, s_xl, s_xr, s_fl, s_fr, s_c, s_w,
    t_p, t_y, t_z, t_x,
    r_c, r_hl, r_hr, r_fl, r_fr, r_z, r_y,
    u_c, u_h, u_f, u_z, u_y, u_o,
):
    chunks, _, block_tokens, width = ty.shape
    toks = block_tokens // NY
    unit = NY * CAP
    block = nz * unit
    half = block // 2
    column = NX * block
    e = lax.axis_index("expert")
    m = lax.axis_index("dp")
    z, y = e // NY, lax.rem(e, NY)
    x, core = m // NC, lax.rem(m, NC)
    other = 1 - core
    xr, xl, xo = lax.rem(x + 1, NX), lax.rem(x + NX - 1, NX), lax.rem(x + 2, NX)
    right, left, partner = (e, xr * NC + core), (e, xl * NC + core), (e, x * NC + other)
    y_peers = [lax.rem(y + d, NY) for d in range(1, NY)]
    z_peers = [lax.rem(z + d, nz) for d in range(1, nz)]

    def at_y(v):
        return (z * NY + v, m)

    def at_z(v):
        return (v * NY + y, m)

    def send(src, dst, ssem, rsem, dev):
        pltpu.make_async_remote_copy(
            src_ref=src, dst_ref=dst, send_sem=ssem, recv_sem=rsem,
            device_id=dev, device_id_type=MESH,
        ).start()

    def local(src, dst, sem):
        pltpu.make_async_copy(src, dst, sem).start()

    def take(ref, sem):
        pltpu.make_async_copy(ref, ref, sem).wait()

    barrier = pltpu.get_barrier_semaphore()
    peers = [at_y(v) for v in y_peers] + [at_z(v) for v in z_peers] + [right, left, partner]
    for dev in peers:
        pl.semaphore_signal(barrier, inc=1, device_id=dev, device_id_type=MESH)

    experts = nz * NY
    few = nz * CAP
    per_device = EXPERTS // experts

    def iota(shape, dim):
        return lax.broadcasted_iota(jnp.int32, shape, dim)

    def ones(mask):
        return jnp.where(mask, 1.0, 0.0)

    cells = (toks, block_tokens)
    place = ones(iota(cells, 1) == iota(cells, 0) + y * toks).astype(BF16)
    ids = mm((idt[...].astype(F32) + 1.0).astype(BF16), place)
    gates = mm(gpr[...], place)
    wanted = (iota((experts, block_tokens), 0) * per_device + 1).astype(F32)
    active = jnp.zeros((experts, block_tokens), F32)
    weight = jnp.zeros((experts, block_tokens), F32)
    for k in range(idt.shape[0]):
        hit = ids[k : k + 1, :] == wanted
        active = active + ones(hit)
        weight = weight + jnp.where(hit, gates[k : k + 1, :], 0.0)
    square = (block_tokens, block_tokens)
    earlier = ones(iota(square, 0) < iota(square, 1)).astype(BF16)
    rank = mm(active.astype(BF16), earlier)
    ordinal = (active * (rank + 1.0)).astype(BF16)
    weight = weight.astype(BF16)
    number = (iota((few, block_tokens), 0) % CAP + 1).astype(F32)
    target = iota((few, experts), 0) // CAP * NY
    for v in range(NY):
        select = ones(iota((few, experts), 1) == target + v).astype(BF16)
        held = mm(select, ordinal) == number
        pp[v, 0] = ones(held).astype(BF16)
        pp[v, 1] = jnp.where(held, mm(select, weight), 0.0).astype(BF16)

    pl.semaphore_wait(barrier, len(peers))
    table = rows_of(y, few)
    for v in y_peers:
        send(pp.at[v], pb.at[:, table], t_p, s_p, at_y(v))
    local(pp.at[y], pb.at[:, table], s_p)

    @pl.loop(0, chunks)
    def _(c):
        cols = rows_of(c, width)
        mine = rows_of(y, toks)
        for a, src in enumerate((tok, og)):
            for v in y_peers:
                send(src.at[:, cols], ty.at[c, a, mine], t_y.at[c], s_y.at[c], at_y(v))
            local(src.at[:, cols], ty.at[c, a, mine], s_y.at[c])

    @pl.loop(0, chunks)
    def _(c):
        cols = rows_of(c, width)
        for i, src in enumerate((wg, wu, wd)):
            local(src.at[:, cols], ww.at[c, i], s_w)

    acc[...] = jnp.zeros_like(acc)
    take(pb, s_p)
    slot = iota((block, block), 0)
    source = slot // CAP % NY * few + slot // unit * CAP + slot % CAP
    spread = ones(iota((block, block), 1) == source).astype(BF16)
    chosen = mm(spread, pb[0])
    pm[...] = chosen.astype(BF16)
    pgm[...] = mm(spread, pb[1]).astype(BF16)
    ptm[...] = chosen.T.astype(BF16)

    mine_rows = rows_of(core * NX + x, block)
    left_rows = rows_of(core * NX + xl, block)
    right_rows = rows_of(core * NX + xr, block)
    opp_rows = rows_of(core * NX + xo, block)
    opp_0 = rows_of((core * NX + xo) * 2, half)
    opp_1 = rows_of((core * NX + xo) * 2 + 1, half)
    left_0 = rows_of((core * NX + xl) * 2, half)
    right_1 = rows_of((core * NX + xr) * 2 + 1, half)
    my_unit = rows_of(z, unit)

    def stage_z(c):
        take(ty.at[c], s_y.at[c])
        zs[c, 0] = mm(pm[...], ty[c, 0]).astype(BF16)
        zs[c, 1] = mm(pgm[...], ty[c, 1]).astype(BF16)
        dst = xg.at[c, :, rows_of((core * NX + x) * nz + z, unit)]
        for v in z_peers:
            send(zs.at[c, :, rows_of(v, unit)], dst, t_z.at[c], s_z.at[c], at_z(v))
        local(zs.at[c, :, my_unit], dst, s_z.at[c])

    def stage_x(c):
        own = xg.at[c, :, mine_rows]
        take(own, s_z.at[c])
        send(own, own, t_x.at[c], s_xl.at[c], right)
        send(own, own, t_x.at[c], s_xr.at[c], left)
        send(own, own, t_x.at[c], s_c.at[c], partner)

    def stage_x2(c):
        from_left = xg.at[c, :, left_rows]
        take(from_left, s_xl.at[c])
        part = xg.at[c, :, left_0]
        send(part, part, t_x.at[c], s_fl.at[c], right)
        send(from_left, from_left, t_x.at[c], s_c.at[c], partner)
        from_right = xg.at[c, :, right_rows]
        take(from_right, s_xr.at[c])
        part = xg.at[c, :, right_1]
        send(part, part, t_x.at[c], s_fr.at[c], left)
        send(from_right, from_right, t_x.at[c], s_c.at[c], partner)

    def stage_x3(c):
        take(xg.at[c, :, opp_0], s_fl.at[c])
        take(xg.at[c, :, opp_1], s_fr.at[c])
        opp = xg.at[c, :, opp_rows]
        send(opp, opp, t_x.at[c], s_c.at[c], partner)

    def stage_f(c):
        @pl.when(c == 0)
        def _():
            take(ww, s_w)

        take(xg.at[c, :, rows_of(other, column)], s_c.at[c])

        @pl.loop(0, NC * NX // 2)
        def _(b):
            rows = rows_of(b, 2 * block)
            xs = xg[c, 0, rows]
            acc[0, rows] += mm_t(xs, ww[c, 0])
            acc[1, rows] += mm_t(xs, ww[c, 1])
            acc[2, rows] += mm_t(xg[c, 1, rows], ww[c, 2])

    stages = ((0, stage_z), (2, stage_x), (5, stage_f), (3, stage_x2), (4, stage_x3))

    @pl.loop(0, chunks + len(stages))
    def _(t):
        for lag, stage in stages:
            c = t - lag

            @pl.when(jnp.logical_and(c >= 0, c < chunks))
            def _(stage=stage, c=c):
                stage(c)

    def activate(rows):
        pre_gate, pre_up, hidden_grad = acc[0, rows], acc[1, rows], acc[2, rows]
        squash = jax.nn.sigmoid(pre_gate)
        activated = pre_gate * squash
        hidden = (activated * pre_up).astype(BF16)
        terms = jnp.sum(hidden.astype(F32) * hidden_grad, axis=1, keepdims=True)
        up_grad = hidden_grad * activated
        gate_grad = hidden_grad * pre_up * squash * (1.0 + pre_gate * (1.0 - squash))
        gp[rows] = gate_grad.astype(BF16)
        up[rows] = up_grad.astype(BF16)
        hd[rows] = hidden
        lane = lax.broadcasted_iota(jnp.int32, (block, LANES), 1)
        return jnp.where(lane == e, terms, 0.0).astype(BF16)

    @pl.loop(0, NX)
    def _(b):
        pse[rows_of(b, block)] = activate(rows_of(other * NX + b, block))
        pke[rows_of(b, block)] = activate(rows_of(core * NX + b, block))

    main = (ps, pk, pr, hl, hr, fl, fr, rs, rz, ts, tr)
    extra = (pse, pke, pre, hle, hre, fle, fre, rse, rze, tse, tre)

    def pick(refs, c):
        return [r.at[c] for r in refs] if refs is main else list(refs)

    def to_partner(refs, c):
        b = pick(refs, c)
        send(b[0], b[2], u_c.at[c], r_c.at[c], partner)

    def stage_pair(c):
        rows = rows_of(other, column)
        ps[c] = (mm(gp[rows], ww[c, 0]) + mm(up[rows], ww[c, 1])).astype(BF16)
        to_partner(main, c)
        rows = rows_of(core, column)
        pk[c] = (mm(gp[rows], ww[c, 0]) + mm(up[rows], ww[c, 1])).astype(BF16)

    def stage_r1(refs, c):
        _, keep, came, to_l, to_r, *_ = pick(refs, c)
        take(came, r_c.at[c])

        @pl.loop(0, NX)
        def _(b):
            rows = rows_of(b, block)
            keep[rows] = (keep[rows].astype(F32) + came[rows].astype(F32)).astype(BF16)

        send(keep.at[rows_of(xo * 2, half)], to_l, u_h.at[c], r_hl.at[c], right)
        send(keep.at[rows_of(xo * 2 + 1, half)], to_r, u_h.at[c], r_hr.at[c], left)

    def stage_r2(refs, c):
        _, keep, _, half_l, half_r, full_l, full_r, *_ = pick(refs, c)
        take(half_l, r_hl.at[c])
        rows = rows_of(xr * 2, half)
        keep[rows] = (keep[rows].astype(F32) + half_l[...].astype(F32)).astype(BF16)
        send(keep.at[rows_of(xr, block)], full_l, u_f.at[c], r_fl.at[c], right)
        take(half_r, r_hr.at[c])
        rows = rows_of(xl * 2 + 1, half)
        keep[rows] = (keep[rows].astype(F32) + half_r[...].astype(F32)).astype(BF16)
        send(keep.at[rows_of(xl, block)], full_r, u_f.at[c], r_fr.at[c], left)

    def stage_r3(refs, c):
        _, keep, _, _, _, full_l, full_r, done, back, *_ = pick(refs, c)
        take(full_l, r_fl.at[c])
        take(full_r, r_fr.at[c])
        done[...] = (
            keep[rows_of(x, block)].astype(F32)
            + full_l[...].astype(F32)
            + full_r[...].astype(F32)
        ).astype(BF16)
        for v in z_peers:
            send(done.at[rows_of(v, unit)], back.at[my_unit], u_z.at[c], r_z.at[c], at_z(v))
        local(done.at[my_unit], back.at[my_unit], r_z.at[c])

    def stage_r4(refs, c):
        *_, back, parts, summed = pick(refs, c)
        take(back, r_z.at[c])
        parts[...] = mm(ptm[...], back[...]).astype(BF16)
        mine = rows_of(y, toks)
        for v in y_peers:
            send(parts.at[rows_of(v, toks)], summed.at[mine], u_y.at[c], r_y.at[c], at_y(v))
        local(parts.at[mine], summed.at[mine], r_y.at[c])

    def stage_r5(refs, c):
        summed = pick(refs, c)[-1]
        take(summed, r_y.at[c])
        out = summed[pl.ds(0, toks)].astype(F32)
        for v in range(1, NY):
            out = out + summed[pl.ds(v * toks, toks)].astype(F32)
        if refs is main:
            tg_out[:, rows_of(c, width)] = out.astype(BF16)
        else:
            gate_terms = out.T
            expert = iota((LANES, toks), 0) * per_device
            for k in range(idt.shape[0]):
                hit = idt[k : k + 1, :] == expert
                term = jnp.sum(jnp.where(hit, gate_terms, 0.0), axis=0, keepdims=True)
                gate_out[k : k + 1, :] = term / gpr[k : k + 1, :].astype(F32)

    def transposes():
        for src, dst in ((gp, gpt), (up, upt), (hd, hdt)):
            @pl.loop(0, NC * NX)
            def _(b, src=src, dst=dst):
                rows = rows_of(b, block)
                dst[:, rows] = src[rows].astype(F32).T.astype(BF16)

    def weight_grads(c):
        cols = rows_of(c, width)
        tokens_c = xg[c, 0]
        go[c, 0] = mm(gpt[...], tokens_c).astype(BF16)
        go[c, 1] = mm(upt[...], tokens_c).astype(BF16)
        go[c, 2] = mm(hdt[...], xg[c, 1]).astype(BF16)
        for i, dst in enumerate((gg_out, gu_out, gd_out)):
            local(go.at[c, i], dst.at[0, :, cols], u_o.at[c, i])

    to_partner(extra, chunks)
    returns = (stage_r1, stage_r2, stage_r3, stage_r4, stage_r5)

    @pl.loop(0, chunks + len(returns))
    def _(t):
        for lag, stage in enumerate(returns):
            @pl.when(t == lag)
            def _(stage=stage):
                stage(extra, chunks)

            c = t - lag - 1

            @pl.when(jnp.logical_and(c >= 0, c < chunks))
            def _(stage=stage, c=c):
                stage(main, c)

        @pl.when(t < chunks)
        def _():
            stage_pair(t)

        @pl.when(t == 2)
        def _():
            transposes()

        @pl.when(jnp.logical_and(t >= 3, t < chunks + 3))
        def _():
            weight_grads(t - 3)

    take(pb.at[:, pl.ds(0, (NY - 1) * few)], t_p)

    def drain(refs, c):
        b = pick(refs, c)
        take(b[0], u_c.at[c])
        take(b[5], u_h.at[c])
        take(b[1].at[pl.ds(0, 2 * block)], u_f.at[c])
        take(b[8].at[pl.ds(0, block - unit)], u_z.at[c])
        take(b[10].at[pl.ds(0, block_tokens - toks)], u_y.at[c])

    drain(extra, chunks)

    @pl.loop(0, chunks)
    def _(c):
        take(ty.at[c, :, pl.ds(0, block_tokens - toks)], t_y.at[c])
        take(zs.at[c, :, pl.ds(0, block - unit)], t_z.at[c])
        take(xg.at[c, :, pl.ds(0, 7 * block)], t_x.at[c])
        drain(main, c)
        cols = rows_of(c, width)
        for i, dst in enumerate((gg_out, gu_out, gd_out)):
            pltpu.make_async_copy(go.at[c, i], dst.at[0, :, cols], u_o.at[c, i]).wait()


def run(tokens, out_grad, ids, gates, w_gate, w_up, w_down, nz):
    toks, depth = tokens.shape
    units = w_gate.shape[0]
    chunks = CHUNKS
    width = depth // chunks
    block = nz * NY * CAP
    total = block * NX * NC
    column = block * NX
    any_spec = pl.BlockSpec(memory_space=pl.ANY)
    vmem_spec = pl.BlockSpec(memory_space=pltpu.VMEM)
    dma = pltpu.SemaphoreType.DMA
    v = pltpu.VMEM

    def back(lead, w):
        return [
            v(lead + (column, w), BF16),
            v(lead + (column, w), BF16),
            v(lead + (column, w), BF16),
            v(lead + (block // 2, w), BF16),
            v(lead + (block // 2, w), BF16),
            v(lead + (block, w), BF16),
            v(lead + (block, w), BF16),
            v(lead + (block, w), BF16),
            v(lead + (block, w), BF16),
            v(lead + (NY * toks, w), BF16),
            v(lead + (NY * toks, w), BF16),
        ]

    scratch = [
        v((NY, 2, nz * CAP, NY * toks), BF16),
        v((2, block, NY * toks), BF16),
        v((block, NY * toks), BF16),
        v((block, NY * toks), BF16),
        v((NY * toks, block), BF16),
        v((chunks, 2, NY * toks, width), BF16),
        v((chunks, 2, block, width), BF16),
        v((chunks, 2, total, width), BF16),
        v((chunks, 3, units, width), BF16),
        v((3, total, units), F32),
        v((total, units), BF16),
        v((total, units), BF16),
        v((total, units), BF16),
        v((units, total), BF16),
        v((units, total), BF16),
        v((units, total), BF16),
        *back((chunks,), width),
        v((chunks, 3, units, width), BF16),
        *back((), LANES),
        dma(()), *[dma((chunks,)) for _ in range(7)], dma(()),
        dma(()), *[dma((chunks,)) for _ in range(3)],
        *[dma((chunks + 1,)) for _ in range(7)],
        *[dma((chunks + 1,)) for _ in range(5)],
        dma((chunks, 3)),
    ]
    grads = jax.ShapeDtypeStruct((1, units, depth), BF16)

    def body(*refs):
        kernel(nz, *refs)

    return pl.pallas_call(
        body,
        out_shape=(
            jax.ShapeDtypeStruct((toks, depth), BF16),
            jax.ShapeDtypeStruct(gates.shape, F32),
            grads, grads, grads,
        ),
        in_specs=[any_spec] * 2 + [vmem_spec] * 2 + [any_spec] * 3,
        out_specs=(vmem_spec, vmem_spec, any_spec, any_spec, any_spec),
        scratch_shapes=scratch,
        compiler_params=pltpu.CompilerParams(
            collective_id=0, has_side_effects=True, vmem_limit_bytes=67043328
        ),
    )(tokens, out_grad, ids, gates, w_gate, w_up, w_down)


def place_kernel(*refs):
    n = (len(refs) - 2) // 3
    srcs, dsts, bufs = refs[:n], refs[n : 2 * n], refs[2 * n : 3 * n]
    came, left = refs[3 * n :]
    for i in range(n):
        pltpu.make_async_copy(srcs[i], bufs[i], came.at[i]).start()
    for i in range(n):
        pltpu.make_async_copy(srcs[i], bufs[i], came.at[i]).wait()
        pltpu.make_async_copy(bufs[i], dsts[i], left.at[i]).start()
    for i in range(n):
        pltpu.make_async_copy(bufs[i], dsts[i], left.at[i]).wait()


def place(*arrays):
    any_spec = pl.BlockSpec(memory_space=pl.ANY)
    return pl.pallas_call(
        place_kernel,
        out_shape=tuple(jax.ShapeDtypeStruct(a.shape, a.dtype) for a in arrays),
        in_specs=[any_spec] * len(arrays),
        out_specs=[any_spec] * len(arrays),
        scratch_shapes=[
            *[pltpu.VMEM(a.shape, a.dtype) for a in arrays],
            pltpu.SemaphoreType.DMA((len(arrays),)),
            pltpu.SemaphoreType.DMA((len(arrays),)),
        ],
    )(*arrays)


def body(tokens, out_grad, gate_probs, route_ids, w_gate, w_up, w_down):
    nz = lax.axis_size("expert") // NY
    token_grad, gate_grad, grad_gate, grad_up, grad_down = run(
        tokens, out_grad, route_ids.T, gate_probs.T, w_gate[0], w_up[0], w_down[0], nz
    )
    token_grad, grad_gate, grad_up, grad_down = place(
        token_grad, grad_gate, grad_up, grad_down
    )
    return token_grad, gate_grad.T, grad_gate, grad_up, grad_down


def solution(mesh):
    in_specs = (
        P(("expert", "dp"), None),
        P(("expert", "dp"), None),
        P(("expert", "dp"), None),
        P(("expert", "dp"), None),
        P("expert", "dp", None),
        P("expert", "dp", None),
        P("expert", "dp", None),
    )
    out_specs = (
        P(("expert", "dp"), None),
        P(("expert", "dp"), None),
        P("expert", "dp", None),
        P("expert", "dp", None),
        P("expert", "dp", None),
    )
    return jax.shard_map(body, mesh=mesh, in_specs=in_specs, out_specs=out_specs, check_vma=False)
```

```python
import jax
import jax.numpy as jnp
from jax import lax
from jax.experimental import pallas as pl
from jax.experimental.pallas import tpu as pltpu
from jax.sharding import PartitionSpec as P

EXPERTS = 128
CAP = 4
NX = 4
NC = 2
NY = 4
CHUNKS = 16
PIECES = 6
LANES = 128
MESH = pl.DeviceIdType.MESH
LAST = (((1,), (1,)), ((), ()))
F32 = jnp.float32
BF16 = jnp.bfloat16


def mm(a, b):
    return jnp.dot(a, b, preferred_element_type=F32)


def mm_t(a, b):
    return lax.dot_general(a, b, LAST, preferred_element_type=F32)


def rows_of(index, size):
    return pl.ds(pl.multiple_of(index * size, size), size)


def kernel(
    nz, tok, og, idt, gpr, wg, wu, wd,
    tg_out, gate_out, gg_out, gu_out, gd_out,
    pp, pb, pm, pgm, ptm, ty, zs, xg, ww, acc, gp, up, hd, gpt, upt, hdt,
    ps, pk, pr, hl, hr, fl, fr, rs, rz, ts, tr, go, tg,
    pse, pke, pre, hle, hre, fle, fre, rse, rze, tse, tre,
    s_p, s_y, s_z, s_xl, s_xr, s_fl, s_fr, s_c, s_w,
    t_p, t_y, t_z, t_x,
    r_c, r_hl, r_hr, r_fl, r_fr, r_z, r_y,
    u_c, u_h, u_f, u_z, u_y, u_o, u_t,
):
    chunks, _, block_tokens, width = ty.shape
    toks = block_tokens // NY
    unit = NY * CAP
    block = nz * unit
    half = block // 2
    column = NX * block
    e = lax.axis_index("expert")
    m = lax.axis_index("dp")
    z, y = e // NY, lax.rem(e, NY)
    x, core = m // NC, lax.rem(m, NC)
    other = 1 - core
    xr, xl, xo = lax.rem(x + 1, NX), lax.rem(x + NX - 1, NX), lax.rem(x + 2, NX)
    right, left, partner = (e, xr * NC + core), (e, xl * NC + core), (e, x * NC + other)
    y_peers = [lax.rem(y + d, NY) for d in range(1, NY)]
    z_peers = [lax.rem(z + d, nz) for d in range(1, nz)]

    def at_y(v):
        return (z * NY + v, m)

    def at_z(v):
        return (v * NY + y, m)

    def send(src, dst, ssem, rsem, dev):
        pltpu.make_async_remote_copy(
            src_ref=src, dst_ref=dst, send_sem=ssem, recv_sem=rsem,
            device_id=dev, device_id_type=MESH,
        ).start()

    def local(src, dst, sem):
        pltpu.make_async_copy(src, dst, sem).start()

    def take(ref, sem):
        pltpu.make_async_copy(ref, ref, sem).wait()

    barrier = pltpu.get_barrier_semaphore()
    peers = [at_y(v) for v in y_peers] + [at_z(v) for v in z_peers] + [right, left, partner]
    for dev in peers:
        pl.semaphore_signal(barrier, inc=1, device_id=dev, device_id_type=MESH)

    experts = nz * NY
    few = nz * CAP
    per_device = EXPERTS // experts

    def iota(shape, dim):
        return lax.broadcasted_iota(jnp.int32, shape, dim)

    def ones(mask):
        return jnp.where(mask, 1.0, 0.0)

    cells = (toks, block_tokens)
    place = ones(iota(cells, 1) == iota(cells, 0) + y * toks).astype(BF16)
    ids = mm((idt[...].astype(F32) + 1.0).astype(BF16), place)
    gates = mm(gpr[...], place)
    wanted = (iota((experts, block_tokens), 0) * per_device + 1).astype(F32)
    active = jnp.zeros((experts, block_tokens), F32)
    weight = jnp.zeros((experts, block_tokens), F32)
    for k in range(idt.shape[0]):
        hit = ids[k : k + 1, :] == wanted
        active = active + ones(hit)
        weight = weight + jnp.where(hit, gates[k : k + 1, :], 0.0)
    square = (block_tokens, block_tokens)
    earlier = ones(iota(square, 0) < iota(square, 1)).astype(BF16)
    rank = mm(active.astype(BF16), earlier)
    ordinal = (active * (rank + 1.0)).astype(BF16)
    weight = weight.astype(BF16)
    number = (iota((few, block_tokens), 0) % CAP + 1).astype(F32)
    target = iota((few, experts), 0) // CAP * NY
    for v in range(NY):
        select = ones(iota((few, experts), 1) == target + v).astype(BF16)
        held = mm(select, ordinal) == number
        pp[v, 0] = ones(held).astype(BF16)
        pp[v, 1] = jnp.where(held, mm(select, weight), 0.0).astype(BF16)

    pl.semaphore_wait(barrier, len(peers))
    table = rows_of(y, few)
    for v in y_peers:
        send(pp.at[v], pb.at[:, table], t_p, s_p, at_y(v))
    local(pp.at[y], pb.at[:, table], s_p)

    @pl.loop(0, chunks)
    def _(c):
        cols = rows_of(c, width)
        mine = rows_of(y, toks)
        for a, src in enumerate((tok, og)):
            for v in y_peers:
                send(src.at[:, cols], ty.at[c, a, mine], t_y.at[c], s_y.at[c], at_y(v))
            local(src.at[:, cols], ty.at[c, a, mine], s_y.at[c])

    @pl.loop(0, chunks)
    def _(c):
        cols = rows_of(c, width)
        for i, src in enumerate((wg, wu, wd)):
            local(src.at[:, cols], ww.at[c, i], s_w)

    acc[...] = jnp.zeros_like(acc)
    take(pb, s_p)
    slot = iota((block, block), 0)
    source = slot // CAP % NY * few + slot // unit * CAP + slot % CAP
    spread = ones(iota((block, block), 1) == source).astype(BF16)
    chosen = mm(spread, pb[0])
    pm[...] = chosen.astype(BF16)
    pgm[...] = mm(spread, pb[1]).astype(BF16)
    ptm[...] = chosen.T.astype(BF16)

    mine_rows = rows_of(core * NX + x, block)
    left_rows = rows_of(core * NX + xl, block)
    right_rows = rows_of(core * NX + xr, block)
    opp_rows = rows_of(core * NX + xo, block)
    opp_0 = rows_of((core * NX + xo) * 2, half)
    opp_1 = rows_of((core * NX + xo) * 2 + 1, half)
    left_0 = rows_of((core * NX + xl) * 2, half)
    right_1 = rows_of((core * NX + xr) * 2 + 1, half)
    my_unit = rows_of(z, unit)

    def stage_z(c):
        take(ty.at[c], s_y.at[c])
        zs[c, 0] = mm(pm[...], ty[c, 0]).astype(BF16)
        zs[c, 1] = mm(pgm[...], ty[c, 1]).astype(BF16)
        dst = xg.at[c, :, rows_of((core * NX + x) * nz + z, unit)]
        for v in z_peers:
            send(zs.at[c, :, rows_of(v, unit)], dst, t_z.at[c], s_z.at[c], at_z(v))
        local(zs.at[c, :, my_unit], dst, s_z.at[c])

    def stage_x(c):
        own = xg.at[c, :, mine_rows]
        take(own, s_z.at[c])
        send(own, own, t_x.at[c], s_xl.at[c], right)
        send(own, own, t_x.at[c], s_xr.at[c], left)
        send(own, own, t_x.at[c], s_c.at[c], partner)

    def stage_x2(c):
        from_left = xg.at[c, :, left_rows]
        take(from_left, s_xl.at[c])
        part = xg.at[c, :, left_0]
        send(part, part, t_x.at[c], s_fl.at[c], right)
        send(from_left, from_left, t_x.at[c], s_c.at[c], partner)
        from_right = xg.at[c, :, right_rows]
        take(from_right, s_xr.at[c])
        part = xg.at[c, :, right_1]
        send(part, part, t_x.at[c], s_fr.at[c], left)
        send(from_right, from_right, t_x.at[c], s_c.at[c], partner)

    def stage_x3(c):
        take(xg.at[c, :, opp_0], s_fl.at[c])
        take(xg.at[c, :, opp_1], s_fr.at[c])
        opp = xg.at[c, :, opp_rows]
        send(opp, opp, t_x.at[c], s_c.at[c], partner)

    def stage_f(c):
        @pl.when(c == 0)
        def _():
            take(ww, s_w)

        take(xg.at[c, :, rows_of(other, column)], s_c.at[c])

        @pl.loop(0, NC * NX // 2)
        def _(b):
            rows = rows_of(b, 2 * block)
            xs = xg[c, 0, rows]
            acc[0, rows] += mm_t(xs, ww[c, 0])
            acc[1, rows] += mm_t(xs, ww[c, 1])
            acc[2, rows] += mm_t(xg[c, 1, rows], ww[c, 2])

    stages = ((0, stage_z), (3, stage_x), (9, stage_f), (5, stage_x2), (7, stage_x3))

    @pl.loop(0, chunks + 9)
    def _(t):
        for lag, stage in stages:
            c = t - lag

            @pl.when(jnp.logical_and(c >= 0, c < chunks))
            def _(stage=stage, c=c):
                stage(c)

    def activate(rows):
        pre_gate, pre_up, hidden_grad = acc[0, rows], acc[1, rows], acc[2, rows]
        squash = jax.nn.sigmoid(pre_gate)
        activated = pre_gate * squash
        hidden = (activated * pre_up).astype(BF16)
        terms = jnp.sum(hidden.astype(F32) * hidden_grad, axis=1, keepdims=True)
        up_grad = hidden_grad * activated
        gate_grad = hidden_grad * pre_up * squash * (1.0 + pre_gate * (1.0 - squash))
        gp[rows] = gate_grad.astype(BF16)
        up[rows] = up_grad.astype(BF16)
        hd[rows] = hidden
        lane = lax.broadcasted_iota(jnp.int32, (block, LANES), 1)
        return jnp.where(lane == e, terms, 0.0).astype(BF16)

    @pl.loop(0, NX)
    def _(b):
        pse[rows_of(b, block)] = activate(rows_of(other * NX + b, block))

    main = (ps, pk, pr, hl, hr, fl, fr, rs, rz, ts, tr)
    extra = (pse, pke, pre, hle, hre, fle, fre, rse, rze, tse, tre)

    def pick(refs, c):
        return [r.at[c] for r in refs] if refs is main else list(refs)

    def to_partner(refs, c):
        b = pick(refs, c)
        send(b[0], b[2], u_c.at[c], r_c.at[c], partner)

    def pair_send(c):
        rows = rows_of(other, column)
        ps[c] = (mm(gp[rows], ww[c, 0]) + mm(up[rows], ww[c, 1])).astype(BF16)
        to_partner(main, c)

    def pair_keep(c):
        rows = rows_of(core, column)
        pk[c] = (mm(gp[rows], ww[c, 0]) + mm(up[rows], ww[c, 1])).astype(BF16)

    def stage_r1(refs, c):
        _, keep, came, to_l, to_r, *_ = pick(refs, c)
        take(came, r_c.at[c])

        @pl.loop(0, NX)
        def _(b):
            rows = rows_of(b, block)
            keep[rows] = (keep[rows].astype(F32) + came[rows].astype(F32)).astype(BF16)

        send(keep.at[rows_of(xo * 2, half)], to_l, u_h.at[c], r_hl.at[c], right)
        send(keep.at[rows_of(xo * 2 + 1, half)], to_r, u_h.at[c], r_hr.at[c], left)

    def stage_r2(refs, c):
        _, keep, _, half_l, half_r, full_l, full_r, *_ = pick(refs, c)
        take(half_l, r_hl.at[c])
        rows = rows_of(xr * 2, half)
        keep[rows] = (keep[rows].astype(F32) + half_l[...].astype(F32)).astype(BF16)
        send(keep.at[rows_of(xr, block)], full_l, u_f.at[c], r_fl.at[c], right)
        take(half_r, r_hr.at[c])
        rows = rows_of(xl * 2 + 1, half)
        keep[rows] = (keep[rows].astype(F32) + half_r[...].astype(F32)).astype(BF16)
        send(keep.at[rows_of(xl, block)], full_r, u_f.at[c], r_fr.at[c], left)

    def stage_r3(refs, c):
        _, keep, _, _, _, full_l, full_r, done, back, *_ = pick(refs, c)
        take(full_l, r_fl.at[c])
        take(full_r, r_fr.at[c])
        done[...] = (
            keep[rows_of(x, block)].astype(F32)
            + full_l[...].astype(F32)
            + full_r[...].astype(F32)
        ).astype(BF16)
        for v in z_peers:
            send(done.at[rows_of(v, unit)], back.at[my_unit], u_z.at[c], r_z.at[c], at_z(v))
        local(done.at[my_unit], back.at[my_unit], r_z.at[c])

    def stage_r4(refs, c):
        *_, back, parts, summed = pick(refs, c)
        take(back, r_z.at[c])
        parts[...] = mm(ptm[...], back[...]).astype(BF16)
        mine = rows_of(y, toks)
        for v in y_peers:
            send(parts.at[rows_of(v, toks)], summed.at[mine], u_y.at[c], r_y.at[c], at_y(v))
        local(parts.at[mine], summed.at[mine], r_y.at[c])

    def stage_r5(refs, c):
        summed = pick(refs, c)[-1]
        take(summed, r_y.at[c])
        out = summed[pl.ds(0, toks)].astype(F32)
        for v in range(1, NY):
            out = out + summed[pl.ds(v * toks, toks)].astype(F32)
        if refs is main:
            tg[c] = out.astype(BF16)
            local(tg.at[c], tg_out.at[:, rows_of(c, width)], u_t.at[c])
        else:
            gate_terms = out.T
            expert = iota((LANES, toks), 0) * per_device
            for k in range(idt.shape[0]):
                hit = idt[k : k + 1, :] == expert
                term = jnp.sum(jnp.where(hit, gate_terms, 0.0), axis=0, keepdims=True)
                gate_out[k : k + 1, :] = term / gpr[k : k + 1, :].astype(F32)

    def transposes():
        for src, dst in ((gp, gpt), (up, upt), (hd, hdt)):
            @pl.loop(0, NC * NX)
            def _(b, src=src, dst=dst):
                rows = rows_of(b, block)
                dst[:, rows] = src[rows].astype(F32).T.astype(BF16)

    def weight_grads(c):
        cols = rows_of(c, width)
        tokens_c = xg[c, 0]
        go[c, 0] = mm(gpt[...], tokens_c).astype(BF16)
        go[c, 1] = mm(upt[...], tokens_c).astype(BF16)
        go[c, 2] = mm(hdt[...], xg[c, 1]).astype(BF16)
        for i, dst in enumerate((gg_out, gu_out, gd_out)):
            local(go.at[c, i], dst.at[0, :, cols], u_o.at[c, i])

    pair_send(0)
    to_partner(extra, chunks)

    @pl.loop(0, NX)
    def _(b):
        pke[rows_of(b, block)] = activate(rows_of(core * NX + b, block))

    returns = ((3, stage_r1), (6, stage_r2), (9, stage_r3), (12, stage_r4), (15, stage_r5))
    turn = 9

    def grads_out(c):
        cols = rows_of(c, width)
        for i, dst in enumerate((gg_out, gu_out, gd_out)):
            pltpu.make_async_copy(go.at[c, i], dst.at[0, :, cols], u_o.at[c, i]).wait()

    def drain(refs, c):
        b = pick(refs, c)
        take(b[0], u_c.at[c])
        take(b[5], u_h.at[c])
        take(b[1].at[pl.ds(0, 2 * block)], u_f.at[c])
        take(b[8].at[pl.ds(0, block - unit)], u_z.at[c])
        take(b[10].at[pl.ds(0, block_tokens - toks)], u_y.at[c])

    @pl.loop(0, chunks + returns[-1][0])
    def _(t):
        for lag, stage in returns:
            @pl.when(t == lag - 1)
            def _(stage=stage):
                stage(extra, chunks)

            c = t - lag

            @pl.when(jnp.logical_and(c >= 0, c < chunks))
            def _(stage=stage, c=c):
                stage(main, c)

        @pl.when(t < chunks)
        def _():
            pair_keep(t)

        @pl.when(t < chunks - 1)
        def _():
            pair_send(t + 1)

        @pl.when(t == turn)
        def _():
            transposes()

        @pl.when(jnp.logical_and(t > turn, t <= chunks // 2 + turn))
        def _():
            weight_grads(2 * (t - turn) - 2)
            weight_grads(2 * (t - turn) - 1)

        @pl.when(jnp.logical_and(t > turn + 2, t <= chunks // 2 + turn + 2))
        def _():
            grads_out(2 * (t - turn - 2) - 2)
            grads_out(2 * (t - turn - 2) - 1)

        @pl.when(t < chunks)
        def _():
            take(ty.at[t, :, pl.ds(0, block_tokens - toks)], t_y.at[t])
            take(zs.at[t, :, pl.ds(0, block - unit)], t_z.at[t])
            take(xg.at[t, :, pl.ds(0, 7 * block)], t_x.at[t])

        done = t - returns[-1][0] - 1

        @pl.when(done >= 0)
        def _():
            drain(main, done)
            pltpu.make_async_copy(
                tg.at[done], tg_out.at[:, rows_of(done, width)], u_t.at[done]
            ).wait()

    take(pb.at[:, pl.ds(0, (NY - 1) * few)], t_p)

    drain(extra, chunks)

    @pl.loop(chunks - 1, chunks)
    def _(c):
        drain(main, c)
        pltpu.make_async_copy(tg.at[c], tg_out.at[:, rows_of(c, width)], u_t.at[c]).wait()


def run(tokens, out_grad, ids, gates, w_gate, w_up, w_down, nz):
    toks, depth = tokens.shape
    units = w_gate.shape[0]
    chunks = CHUNKS
    width = depth // chunks
    block = nz * NY * CAP
    total = block * NX * NC
    column = block * NX
    any_spec = pl.BlockSpec(memory_space=pl.ANY)
    vmem_spec = pl.BlockSpec(memory_space=pltpu.VMEM)
    dma = pltpu.SemaphoreType.DMA
    v = pltpu.VMEM

    def back(lead, w):
        return [
            v(lead + (column, w), BF16),
            v(lead + (column, w), BF16),
            v(lead + (column, w), BF16),
            v(lead + (block // 2, w), BF16),
            v(lead + (block // 2, w), BF16),
            v(lead + (block, w), BF16),
            v(lead + (block, w), BF16),
            v(lead + (block, w), BF16),
            v(lead + (block, w), BF16),
            v(lead + (NY * toks, w), BF16),
            v(lead + (NY * toks, w), BF16),
        ]

    scratch = [
        v((NY, 2, nz * CAP, NY * toks), BF16),
        v((2, block, NY * toks), BF16),
        v((block, NY * toks), BF16),
        v((block, NY * toks), BF16),
        v((NY * toks, block), BF16),
        v((chunks, 2, NY * toks, width), BF16),
        v((chunks, 2, block, width), BF16),
        v((chunks, 2, total, width), BF16),
        v((chunks, 3, units, width), BF16),
        v((3, total, units), F32),
        v((total, units), BF16),
        v((total, units), BF16),
        v((total, units), BF16),
        v((units, total), BF16),
        v((units, total), BF16),
        v((units, total), BF16),
        *back((chunks,), width),
        v((chunks, 3, units, width), BF16),
        v((chunks, toks, width), BF16),
        *back((), LANES),
        dma(()), *[dma((chunks,)) for _ in range(7)], dma(()),
        dma(()), *[dma((chunks,)) for _ in range(3)],
        *[dma((chunks + 1,)) for _ in range(7)],
        *[dma((chunks + 1,)) for _ in range(5)],
        dma((chunks, 3)),
        dma((chunks,)),
    ]
    grads = jax.ShapeDtypeStruct((1, units, depth), BF16)

    def body(*refs):
        kernel(nz, *refs)

    return pl.pallas_call(
        body,
        out_shape=(
            jax.ShapeDtypeStruct((toks, depth), BF16),
            jax.ShapeDtypeStruct(gates.shape, F32),
            grads, grads, grads,
        ),
        in_specs=[any_spec] * 2 + [vmem_spec] * 2 + [any_spec] * 3,
        out_specs=(any_spec, vmem_spec, any_spec, any_spec, any_spec),
        scratch_shapes=scratch,
        compiler_params=pltpu.CompilerParams(
            collective_id=0, has_side_effects=True, vmem_limit_bytes=67043328
        ),
    )(tokens, out_grad, ids, gates, w_gate, w_up, w_down)


def place_kernel(*refs):
    n = (len(refs) - 2) // 3
    srcs, dsts, bufs = refs[:n], refs[n : 2 * n], refs[2 * n : 3 * n]
    came, left = refs[3 * n :]
    jobs = []
    for i in range(n):
        rows = srcs[i].shape[-2]
        step = max(32, rows // PIECES)
        for low in range(0, rows, step):
            piece = (slice(None),) * (len(srcs[i].shape) - 2) + (pl.ds(low, step),)
            jobs.append((srcs[i].at[piece], bufs[i].at[piece], dsts[i].at[piece]))
    for k, (src, buf, _) in enumerate(jobs):
        pltpu.make_async_copy(src, buf, came.at[k]).start()
    for k, (src, buf, dst) in enumerate(jobs):
        pltpu.make_async_copy(src, buf, came.at[k]).wait()
        pltpu.make_async_copy(buf, dst, left.at[k]).start()
    for k, (_, buf, dst) in enumerate(jobs):
        pltpu.make_async_copy(buf, dst, left.at[k]).wait()


def place(*arrays):
    any_spec = pl.BlockSpec(memory_space=pl.ANY)
    return pl.pallas_call(
        place_kernel,
        out_shape=tuple(jax.ShapeDtypeStruct(a.shape, a.dtype) for a in arrays),
        in_specs=[any_spec] * len(arrays),
        out_specs=[any_spec] * len(arrays),
        scratch_shapes=[
            *[pltpu.VMEM(a.shape, a.dtype) for a in arrays],
            pltpu.SemaphoreType.DMA((len(arrays) * PIECES,)),
            pltpu.SemaphoreType.DMA((len(arrays) * PIECES,)),
        ],
    )(*arrays)


def body(tokens, out_grad, gate_probs, route_ids, w_gate, w_up, w_down):
    nz = lax.axis_size("expert") // NY
    token_grad, gate_grad, grad_gate, grad_up, grad_down = run(
        tokens, out_grad, route_ids.T, gate_probs.T, w_gate[0], w_up[0], w_down[0], nz
    )
    token_grad, grad_gate, grad_up, grad_down = place(
        token_grad, grad_gate, grad_up, grad_down
    )
    return token_grad, gate_grad.T, grad_gate, grad_up, grad_down


def solution(mesh):
    in_specs = (
        P(("expert", "dp"), None),
        P(("expert", "dp"), None),
        P(("expert", "dp"), None),
        P(("expert", "dp"), None),
        P("expert", "dp", None),
        P("expert", "dp", None),
        P("expert", "dp", None),
    )
    out_specs = (
        P(("expert", "dp"), None),
        P(("expert", "dp"), None),
        P("expert", "dp", None),
        P("expert", "dp", None),
        P("expert", "dp", None),
    )
    return jax.shard_map(body, mesh=mesh, in_specs=in_specs, out_specs=out_specs, check_vma=False)
```

```python
import jax
import jax.numpy as jnp
from jax import lax
from jax.experimental import pallas as pl
from jax.experimental.pallas import tpu as pltpu
from jax.sharding import PartitionSpec as P

EXPERTS = 128
CAP = 4
NX = 4
NC = 2
NY = 4
CHUNKS = 16
PIECES = 1
LANES = 128
MESH = pl.DeviceIdType.MESH
LAST = (((1,), (1,)), ((), ()))
F32 = jnp.float32
BF16 = jnp.bfloat16


def mm(a, b):
    return jnp.dot(a, b, preferred_element_type=F32)


def mm_t(a, b):
    return lax.dot_general(a, b, LAST, preferred_element_type=F32)


def rows_of(index, size):
    return pl.ds(pl.multiple_of(index * size, size), size)


def kernel(
    nz, tok, og, idt, gpr, wg, wu, wd,
    tg_out, gate_out, gg_out, gu_out, gd_out,
    pp, pb, pm, pgm, ptm, ty, zs, xg, ww, acc, gp, up, hd, gpt, upt, hdt,
    ps, pk, pr, hl, hr, fl, fr, rs, rz, ts, tr, go, tg,
    pse, pke, pre, hle, hre, fle, fre, rse, rze, tse, tre,
    s_p, s_y, s_z, s_xl, s_xr, s_fl, s_fr, s_c, s_w,
    t_p, t_y, t_z, t_x,
    r_c, r_hl, r_hr, r_fl, r_fr, r_z, r_y,
    u_c, u_h, u_f, u_z, u_y, u_o, u_t,
):
    chunks, _, block_tokens, width = ty.shape
    toks = block_tokens // NY
    unit = NY * CAP
    block = nz * unit
    half = block // 2
    column = NX * block
    e = lax.axis_index("expert")
    m = lax.axis_index("dp")
    z, y = e // NY, lax.rem(e, NY)
    x, core = m // NC, lax.rem(m, NC)
    other = 1 - core
    xr, xl, xo = lax.rem(x + 1, NX), lax.rem(x + NX - 1, NX), lax.rem(x + 2, NX)
    right, left, partner = (e, xr * NC + core), (e, xl * NC + core), (e, x * NC + other)
    y_peers = [lax.rem(y + d, NY) for d in range(1, NY)]
    z_peers = [lax.rem(z + d, nz) for d in range(1, nz)]

    def at_y(v):
        return (z * NY + v, m)

    def at_z(v):
        return (v * NY + y, m)

    def send(src, dst, ssem, rsem, dev):
        pltpu.make_async_remote_copy(
            src_ref=src, dst_ref=dst, send_sem=ssem, recv_sem=rsem,
            device_id=dev, device_id_type=MESH,
        ).start()

    def local(src, dst, sem):
        pltpu.make_async_copy(src, dst, sem).start()

    def take(ref, sem):
        pltpu.make_async_copy(ref, ref, sem).wait()

    barrier = pltpu.get_barrier_semaphore()
    peers = [at_y(v) for v in y_peers] + [at_z(v) for v in z_peers] + [right, left, partner]
    for dev in peers:
        pl.semaphore_signal(barrier, inc=1, device_id=dev, device_id_type=MESH)

    experts = nz * NY
    few = nz * CAP
    per_device = EXPERTS // experts

    def iota(shape, dim):
        return lax.broadcasted_iota(jnp.int32, shape, dim)

    def ones(mask):
        return jnp.where(mask, 1.0, 0.0)

    cells = (toks, block_tokens)
    place = ones(iota(cells, 1) == iota(cells, 0) + y * toks).astype(BF16)
    ids = mm((idt[...].astype(F32) + 1.0).astype(BF16), place)
    gates = mm(gpr[...], place)
    wanted = (iota((experts, block_tokens), 0) * per_device + 1).astype(F32)
    active = jnp.zeros((experts, block_tokens), F32)
    weight = jnp.zeros((experts, block_tokens), F32)
    for k in range(idt.shape[0]):
        hit = ids[k : k + 1, :] == wanted
        active = active + ones(hit)
        weight = weight + jnp.where(hit, gates[k : k + 1, :], 0.0)
    square = (block_tokens, block_tokens)
    earlier = ones(iota(square, 0) < iota(square, 1)).astype(BF16)
    rank = mm(active.astype(BF16), earlier)
    ordinal = (active * (rank + 1.0)).astype(BF16)
    weight = weight.astype(BF16)
    number = (iota((few, block_tokens), 0) % CAP + 1).astype(F32)
    target = iota((few, experts), 0) // CAP * NY
    for v in range(NY):
        select = ones(iota((few, experts), 1) == target + v).astype(BF16)
        held = mm(select, ordinal) == number
        pp[v, 0] = ones(held).astype(BF16)
        pp[v, 1] = jnp.where(held, mm(select, weight), 0.0).astype(BF16)

    pl.semaphore_wait(barrier, len(peers))
    table = rows_of(y, few)
    for v in y_peers:
        send(pp.at[v], pb.at[:, table], t_p, s_p, at_y(v))
    local(pp.at[y], pb.at[:, table], s_p)

    @pl.loop(0, chunks)
    def _(c):
        cols = rows_of(c, width)
        mine = rows_of(y, toks)
        for a, src in enumerate((tok, og)):
            for v in y_peers:
                send(src.at[:, cols], ty.at[c, a, mine], t_y.at[c], s_y.at[c], at_y(v))
            local(src.at[:, cols], ty.at[c, a, mine], s_y.at[c])

    @pl.loop(0, chunks)
    def _(c):
        cols = rows_of(c, width)
        for i, src in enumerate((wg, wu, wd)):
            local(src.at[:, cols], ww.at[c, i], s_w)

    acc[...] = jnp.zeros_like(acc)
    take(pb, s_p)
    slot = iota((block, block), 0)
    source = slot // CAP % NY * few + slot // unit * CAP + slot % CAP
    spread = ones(iota((block, block), 1) == source).astype(BF16)
    chosen = mm(spread, pb[0])
    pm[...] = chosen.astype(BF16)
    pgm[...] = mm(spread, pb[1]).astype(BF16)
    ptm[...] = chosen.T.astype(BF16)

    mine_rows = rows_of(core * NX + x, block)
    left_rows = rows_of(core * NX + xl, block)
    right_rows = rows_of(core * NX + xr, block)
    opp_rows = rows_of(core * NX + xo, block)
    opp_0 = rows_of((core * NX + xo) * 2, half)
    opp_1 = rows_of((core * NX + xo) * 2 + 1, half)
    left_0 = rows_of((core * NX + xl) * 2, half)
    right_1 = rows_of((core * NX + xr) * 2 + 1, half)
    my_unit = rows_of(z, unit)

    def stage_z(c):
        take(ty.at[c], s_y.at[c])
        zs[c, 0] = mm(pm[...], ty[c, 0]).astype(BF16)
        zs[c, 1] = mm(pgm[...], ty[c, 1]).astype(BF16)
        dst = xg.at[c, :, rows_of((core * NX + x) * nz + z, unit)]
        for v in z_peers:
            send(zs.at[c, :, rows_of(v, unit)], dst, t_z.at[c], s_z.at[c], at_z(v))
        local(zs.at[c, :, my_unit], dst, s_z.at[c])

    def stage_x(c):
        own = xg.at[c, :, mine_rows]
        take(own, s_z.at[c])
        send(own, own, t_x.at[c], s_xl.at[c], right)
        send(own, own, t_x.at[c], s_xr.at[c], left)
        send(own, own, t_x.at[c], s_c.at[c], partner)

    def stage_x2(c):
        from_left = xg.at[c, :, left_rows]
        take(from_left, s_xl.at[c])
        part = xg.at[c, :, left_0]
        send(part, part, t_x.at[c], s_fl.at[c], right)
        send(from_left, from_left, t_x.at[c], s_c.at[c], partner)
        from_right = xg.at[c, :, right_rows]
        take(from_right, s_xr.at[c])
        part = xg.at[c, :, right_1]
        send(part, part, t_x.at[c], s_fr.at[c], left)
        send(from_right, from_right, t_x.at[c], s_c.at[c], partner)

    def stage_x3(c):
        take(xg.at[c, :, opp_0], s_fl.at[c])
        take(xg.at[c, :, opp_1], s_fr.at[c])
        opp = xg.at[c, :, opp_rows]
        send(opp, opp, t_x.at[c], s_c.at[c], partner)

    def stage_f(c):
        @pl.when(c == 0)
        def _():
            take(ww, s_w)

        take(xg.at[c, :, rows_of(other, column)], s_c.at[c])

        @pl.loop(0, NC * NX // 2)
        def _(b):
            rows = rows_of(b, 2 * block)
            xs = xg[c, 0, rows]
            acc[0, rows] += mm_t(xs, ww[c, 0])
            acc[1, rows] += mm_t(xs, ww[c, 1])
            acc[2, rows] += mm_t(xg[c, 1, rows], ww[c, 2])

    stages = ((0, stage_z), (3, stage_x), (9, stage_f), (5, stage_x2), (7, stage_x3))

    @pl.loop(0, chunks + 9)
    def _(t):
        for lag, stage in stages:
            c = t - lag

            @pl.when(jnp.logical_and(c >= 0, c < chunks))
            def _(stage=stage, c=c):
                stage(c)

    def activate(rows):
        pre_gate, pre_up, hidden_grad = acc[0, rows], acc[1, rows], acc[2, rows]
        squash = jax.nn.sigmoid(pre_gate)
        activated = pre_gate * squash
        hidden = (activated * pre_up).astype(BF16)
        terms = jnp.sum(hidden.astype(F32) * hidden_grad, axis=1, keepdims=True)
        up_grad = hidden_grad * activated
        gate_grad = hidden_grad * pre_up * squash * (1.0 + pre_gate * (1.0 - squash))
        gp[rows] = gate_grad.astype(BF16)
        up[rows] = up_grad.astype(BF16)
        hd[rows] = hidden
        lane = lax.broadcasted_iota(jnp.int32, (block, LANES), 1)
        return jnp.where(lane == e, terms, 0.0).astype(BF16)

    @pl.loop(0, NX)
    def _(b):
        pse[rows_of(b, block)] = activate(rows_of(other * NX + b, block))

    main = (ps, pk, pr, hl, hr, fl, fr, rs, rz, ts, tr)
    extra = (pse, pke, pre, hle, hre, fle, fre, rse, rze, tse, tre)

    def pick(refs, c):
        return [r.at[c] for r in refs] if refs is main else list(refs)

    def to_partner(refs, c):
        b = pick(refs, c)
        send(b[0], b[2], u_c.at[c], r_c.at[c], partner)

    def pair_send(c):
        rows = rows_of(other, column)
        ps[c] = (mm(gp[rows], ww[c, 0]) + mm(up[rows], ww[c, 1])).astype(BF16)
        to_partner(main, c)

    def pair_keep(c):
        rows = rows_of(core, column)
        pk[c] = (mm(gp[rows], ww[c, 0]) + mm(up[rows], ww[c, 1])).astype(BF16)

    def stage_r1(refs, c):
        _, keep, came, to_l, to_r, *_ = pick(refs, c)
        take(came, r_c.at[c])

        @pl.loop(0, NX)
        def _(b):
            rows = rows_of(b, block)
            keep[rows] = (keep[rows].astype(F32) + came[rows].astype(F32)).astype(BF16)

        send(keep.at[rows_of(xo * 2, half)], to_l, u_h.at[c], r_hl.at[c], right)
        send(keep.at[rows_of(xo * 2 + 1, half)], to_r, u_h.at[c], r_hr.at[c], left)

    def stage_r2(refs, c):
        _, keep, _, half_l, half_r, full_l, full_r, *_ = pick(refs, c)
        take(half_l, r_hl.at[c])
        rows = rows_of(xr * 2, half)
        keep[rows] = (keep[rows].astype(F32) + half_l[...].astype(F32)).astype(BF16)
        send(keep.at[rows_of(xr, block)], full_l, u_f.at[c], r_fl.at[c], right)
        take(half_r, r_hr.at[c])
        rows = rows_of(xl * 2 + 1, half)
        keep[rows] = (keep[rows].astype(F32) + half_r[...].astype(F32)).astype(BF16)
        send(keep.at[rows_of(xl, block)], full_r, u_f.at[c], r_fr.at[c], left)

    def stage_r3(refs, c):
        _, keep, _, _, _, full_l, full_r, done, back, *_ = pick(refs, c)
        take(full_l, r_fl.at[c])
        take(full_r, r_fr.at[c])
        done[...] = (
            keep[rows_of(x, block)].astype(F32)
            + full_l[...].astype(F32)
            + full_r[...].astype(F32)
        ).astype(BF16)
        for v in z_peers:
            send(done.at[rows_of(v, unit)], back.at[my_unit], u_z.at[c], r_z.at[c], at_z(v))
        local(done.at[my_unit], back.at[my_unit], r_z.at[c])

    def stage_r4(refs, c):
        *_, back, parts, summed = pick(refs, c)
        take(back, r_z.at[c])
        parts[...] = mm(ptm[...], back[...]).astype(BF16)
        mine = rows_of(y, toks)
        for v in y_peers:
            send(parts.at[rows_of(v, toks)], summed.at[mine], u_y.at[c], r_y.at[c], at_y(v))
        local(parts.at[mine], summed.at[mine], r_y.at[c])

    def stage_r5(refs, c):
        summed = pick(refs, c)[-1]
        take(summed, r_y.at[c])
        out = summed[pl.ds(0, toks)].astype(F32)
        for v in range(1, NY):
            out = out + summed[pl.ds(v * toks, toks)].astype(F32)
        if refs is main:
            tg[c] = out.astype(BF16)
            local(tg.at[c], tg_out.at[:, rows_of(c, width)], u_t.at[c])
        else:
            gate_terms = out.T
            expert = iota((LANES, toks), 0) * per_device
            for k in range(idt.shape[0]):
                hit = idt[k : k + 1, :] == expert
                term = jnp.sum(jnp.where(hit, gate_terms, 0.0), axis=0, keepdims=True)
                gate_out[k : k + 1, :] = term / gpr[k : k + 1, :].astype(F32)

    def transposes():
        for src, dst in ((gp, gpt), (up, upt), (hd, hdt)):
            @pl.loop(0, NC * NX)
            def _(b, src=src, dst=dst):
                rows = rows_of(b, block)
                dst[:, rows] = src[rows].astype(F32).T.astype(BF16)

    def weight_grads(c):
        cols = rows_of(c, width)
        tokens_c = xg[c, 0]
        go[c, 0] = mm(gpt[...], tokens_c).astype(BF16)
        go[c, 1] = mm(upt[...], tokens_c).astype(BF16)
        go[c, 2] = mm(hdt[...], xg[c, 1]).astype(BF16)
        for i, dst in enumerate((gg_out, gu_out, gd_out)):
            local(go.at[c, i], dst.at[0, :, cols], u_o.at[c, i])

    pair_send(0)
    to_partner(extra, chunks)

    @pl.loop(0, NX)
    def _(b):
        pke[rows_of(b, block)] = activate(rows_of(core * NX + b, block))

    returns = ((3, stage_r1), (6, stage_r2), (9, stage_r3), (12, stage_r4), (15, stage_r5))
    turn = 9

    def grads_out(c):
        cols = rows_of(c, width)
        for i, dst in enumerate((gg_out, gu_out, gd_out)):
            pltpu.make_async_copy(go.at[c, i], dst.at[0, :, cols], u_o.at[c, i]).wait()

    def drain(refs, c):
        b = pick(refs, c)
        take(b[0], u_c.at[c])
        take(b[5], u_h.at[c])
        take(b[1].at[pl.ds(0, 2 * block)], u_f.at[c])
        take(b[8].at[pl.ds(0, block - unit)], u_z.at[c])
        take(b[10].at[pl.ds(0, block_tokens - toks)], u_y.at[c])

    @pl.loop(0, chunks + returns[-1][0])
    def _(t):
        for lag, stage in returns:
            @pl.when(t == lag - 1)
            def _(stage=stage):
                stage(extra, chunks)

            c = t - lag

            @pl.when(jnp.logical_and(c >= 0, c < chunks))
            def _(stage=stage, c=c):
                stage(main, c)

        @pl.when(t < chunks)
        def _():
            pair_keep(t)

        @pl.when(t < chunks - 1)
        def _():
            pair_send(t + 1)

        @pl.when(t == turn)
        def _():
            transposes()

        @pl.when(jnp.logical_and(t > turn, t <= chunks // 2 + turn))
        def _():
            weight_grads(2 * (t - turn) - 2)
            weight_grads(2 * (t - turn) - 1)

        @pl.when(jnp.logical_and(t > turn + 2, t <= chunks // 2 + turn + 2))
        def _():
            grads_out(2 * (t - turn - 2) - 2)
            grads_out(2 * (t - turn - 2) - 1)

        @pl.when(t < chunks)
        def _():
            take(ty.at[t, :, pl.ds(0, block_tokens - toks)], t_y.at[t])
            take(zs.at[t, :, pl.ds(0, block - unit)], t_z.at[t])
            take(xg.at[t, :, pl.ds(0, 7 * block)], t_x.at[t])

        done = t - returns[-1][0] - 1

        @pl.when(done >= 0)
        def _():
            drain(main, done)
            pltpu.make_async_copy(
                tg.at[done], tg_out.at[:, rows_of(done, width)], u_t.at[done]
            ).wait()

    take(pb.at[:, pl.ds(0, (NY - 1) * few)], t_p)

    drain(extra, chunks)

    @pl.loop(chunks - 1, chunks)
    def _(c):
        drain(main, c)
        pltpu.make_async_copy(tg.at[c], tg_out.at[:, rows_of(c, width)], u_t.at[c]).wait()


def run(tokens, out_grad, ids, gates, w_gate, w_up, w_down, nz):
    toks, depth = tokens.shape
    units = w_gate.shape[0]
    chunks = CHUNKS
    width = depth // chunks
    block = nz * NY * CAP
    total = block * NX * NC
    column = block * NX
    any_spec = pl.BlockSpec(memory_space=pl.ANY)
    vmem_spec = pl.BlockSpec(memory_space=pltpu.VMEM)
    dma = pltpu.SemaphoreType.DMA
    v = pltpu.VMEM

    def back(lead, w):
        return [
            v(lead + (column, w), BF16),
            v(lead + (column, w), BF16),
            v(lead + (column, w), BF16),
            v(lead + (block // 2, w), BF16),
            v(lead + (block // 2, w), BF16),
            v(lead + (block, w), BF16),
            v(lead + (block, w), BF16),
            v(lead + (block, w), BF16),
            v(lead + (block, w), BF16),
            v(lead + (NY * toks, w), BF16),
            v(lead + (NY * toks, w), BF16),
        ]

    scratch = [
        v((NY, 2, nz * CAP, NY * toks), BF16),
        v((2, block, NY * toks), BF16),
        v((block, NY * toks), BF16),
        v((block, NY * toks), BF16),
        v((NY * toks, block), BF16),
        v((chunks, 2, NY * toks, width), BF16),
        v((chunks, 2, block, width), BF16),
        v((chunks, 2, total, width), BF16),
        v((chunks, 3, units, width), BF16),
        v((3, total, units), F32),
        v((total, units), BF16),
        v((total, units), BF16),
        v((total, units), BF16),
        v((units, total), BF16),
        v((units, total), BF16),
        v((units, total), BF16),
        *back((chunks,), width),
        v((chunks, 3, units, width), BF16),
        v((chunks, toks, width), BF16),
        *back((), LANES),
        dma(()), *[dma((chunks,)) for _ in range(7)], dma(()),
        dma(()), *[dma((chunks,)) for _ in range(3)],
        *[dma((chunks + 1,)) for _ in range(7)],
        *[dma((chunks + 1,)) for _ in range(5)],
        dma((chunks, 3)),
        dma((chunks,)),
    ]
    grads = jax.ShapeDtypeStruct((1, units, depth), BF16)

    def body(*refs):
        kernel(nz, *refs)

    return pl.pallas_call(
        body,
        out_shape=(
            jax.ShapeDtypeStruct((toks, depth), BF16),
            jax.ShapeDtypeStruct(gates.shape, F32),
            grads, grads, grads,
        ),
        in_specs=[any_spec] * 2 + [vmem_spec] * 2 + [any_spec] * 3,
        out_specs=(any_spec, vmem_spec, any_spec, any_spec, any_spec),
        scratch_shapes=scratch,
        compiler_params=pltpu.CompilerParams(
            collective_id=0, has_side_effects=True, vmem_limit_bytes=67043328
        ),
    )(tokens, out_grad, ids, gates, w_gate, w_up, w_down)


def place_kernel(*refs):
    n = (len(refs) - 2) // 3
    srcs, dsts, bufs = refs[:n], refs[n : 2 * n], refs[2 * n : 3 * n]
    came, left = refs[3 * n :]
    jobs = []
    for i in range(n):
        rows = srcs[i].shape[-2]
        step = max(32, rows // PIECES)
        for low in range(0, rows, step):
            piece = (slice(None),) * (len(srcs[i].shape) - 2) + (pl.ds(low, step),)
            jobs.append((srcs[i].at[piece], bufs[i].at[piece], dsts[i].at[piece]))
    for k, (src, buf, _) in enumerate(jobs):
        pltpu.make_async_copy(src, buf, came.at[k]).start()
    for k, (src, buf, dst) in enumerate(jobs):
        pltpu.make_async_copy(src, buf, came.at[k]).wait()
        pltpu.make_async_copy(buf, dst, left.at[k]).start()
    for k, (_, buf, dst) in enumerate(jobs):
        pltpu.make_async_copy(buf, dst, left.at[k]).wait()


def place(*arrays):
    any_spec = pl.BlockSpec(memory_space=pl.ANY)
    return pl.pallas_call(
        place_kernel,
        out_shape=tuple(jax.ShapeDtypeStruct(a.shape, a.dtype) for a in arrays),
        in_specs=[any_spec] * len(arrays),
        out_specs=[any_spec] * len(arrays),
        scratch_shapes=[
            *[pltpu.VMEM(a.shape, a.dtype) for a in arrays],
            pltpu.SemaphoreType.DMA((len(arrays) * PIECES,)),
            pltpu.SemaphoreType.DMA((len(arrays) * PIECES,)),
        ],
    )(*arrays)


def body(tokens, out_grad, gate_probs, route_ids, w_gate, w_up, w_down):
    nz = lax.axis_size("expert") // NY
    token_grad, gate_grad, grad_gate, grad_up, grad_down = run(
        tokens, out_grad, route_ids.T, gate_probs.T, w_gate[0], w_up[0], w_down[0], nz
    )
    token_grad, grad_gate, grad_up, grad_down = place(
        token_grad, grad_gate, grad_up, grad_down
    )
    return token_grad, gate_grad.T, grad_gate, grad_up, grad_down


def solution(mesh):
    in_specs = (
        P(("expert", "dp"), None),
        P(("expert", "dp"), None),
        P(("expert", "dp"), None),
        P(("expert", "dp"), None),
        P("expert", "dp", None),
        P("expert", "dp", None),
        P("expert", "dp", None),
    )
    out_specs = (
        P(("expert", "dp"), None),
        P(("expert", "dp"), None),
        P("expert", "dp", None),
        P("expert", "dp", None),
        P("expert", "dp", None),
    )
    return jax.shard_map(body, mesh=mesh, in_specs=in_specs, out_specs=out_specs, check_vma=False)
```
